512 devices in a mesh: depth: 16 (over y_hi, z), illum: 32 (over x, y_lo, core).
Axes of the slice: x: 4, y: 8 (y_hi: 2, y_lo: 4; y = y_hi * 4 + y_lo), z: 8, core: 2. Of those that a mesh axis runs over, the one named last changes fastest.
Arguments:
- amplitude: float32 [16, 256, 256], P('depth', 'illum'), may hold values from 0.92 to 1
- phase: float32 [16, 256, 256], P('depth', 'illum'), may hold values from -3.140625 to 3.140625
- kernel_phase: float32 [256, 256], replicated, may hold values from -3.140625 to 3.140625
- entry_field: float32 [2, 16, 32, 256, 256], P(None, 'depth', 'illum'), may hold values from -6 to 6
- cotangent: float32 [2, 32, 256, 256], P(None, 'illum'), may hold values from -6 to 6
Outputs:
- slice_grad: float32 [2, 16, 256, 256], P(None, 'depth', 'illum')
The draws below stay inside these ranges and needn't reach their ends.
All inputs are finite; a program needn't handle non-finite values.
Results may differ from the reference program's by a relative error of at most 0.0003.
Values sent between devices are 32-bit elements; how exact they have to be, the bound alone decides.
No kernel may reach another device: no remote copies, remote signals or barrier semaphores. Data moves between devices by JAX's collectives and lax.ppermute only.
A program may use at most 64 MiB of HBM per device.

```python
import math
import jax
import jax.numpy as jnp
from jax import lax

GRID = 256
SLICE_DEV = 1
BLOCKS = 16
SLICES = 16
ANGLES = 32


def spiked(entries, key, source, target, blocks, factor):
    owner, partner = [(jnp.arange(entries.shape[position]) // (entries.shape[position] // blocks)).reshape([-1 if axis == position else 1 for axis in range(entries.ndim)]) for position in (source, target)]
    chosen = jax.random.permutation(key, blocks)[partner]
    strong = (owner == chosen) | (owner == (partner + blocks // 2) % blocks)
    return jnp.where(strong, factor * entries, entries)


def steps_of(key, extent, pieces, low, top_value):
    level = 1.0
    for axis_at, shards_of in pieces:
        steps = jax.random.uniform(jax.random.fold_in(jax.random.fold_in(key, 6), axis_at), (shards_of,), jnp.float32, low / len(pieces), top_value / len(pieces))
        level = level * jnp.repeat(jnp.exp(steps), extent[axis_at] // shards_of).reshape((-1,) + (1,) * (len(extent) - 1 - axis_at))
    return level


def scatter_about(rng, dims, spread, most, shards=(), dtype=jnp.bfloat16):
    gain = steps_of(rng, dims, shards, -0.22, 0.18) if shards else 1.0
    values = jax.random.normal(rng, dims, jnp.float32) * spread * gain
    return jnp.minimum(jnp.maximum(values, -most), most).astype(dtype)


def heavy_noise(rng, dims, deviation, limit, shards, heavy, held_as=jnp.bfloat16):
    values = deviation * jax.random.normal(rng, dims, jnp.float32)
    if shards:
        values = values * steps_of(rng, dims, shards, -0.22, 0.18)
    return jnp.clip(spiked(values, jax.random.fold_in(rng, 3), *heavy), -limit, limit).astype(held_as)


def setup_inputs(seed: int = 0) -> dict:
    keys = jax.random.split(jax.random.key(seed), 6)
    return {
        "amplitude": jnp.clip(0.92 + 0.07999998 * jax.random.uniform(keys[0], (SLICES, GRID, GRID), jnp.float32) ** steps_of(keys[0], (SLICES, GRID, GRID), ((0, 16), (1, 32)), -0.2, 0.2), 0.92, 1.0),
        "phase": jnp.clip(jax.random.uniform(keys[1], (SLICES, GRID, GRID), jnp.float32, -3.140625, 3.140625), -3.140625, 3.140625),
        "kernel_phase": jnp.clip(jax.random.uniform(keys[2], (GRID, GRID), jnp.float32, -3.140625, 3.140625), -3.140625, 3.140625),
        "entry_field": scatter_about(keys[3], (2, BLOCKS, ANGLES, GRID, GRID), 1.0, 6.0, ((1, 16), (2, 32)), jnp.float32),
        "cotangent": heavy_noise(keys[4], (2, ANGLES, GRID, GRID), 1.0, 6.0, ((1, 32),), (1, 2, 32, 2.75), jnp.float32),
    }


def propagate(field, kernel):
    return jnp.fft.ifft2(kernel * jnp.fft.fft2(field))

def reference(amplitude, phase, kernel_phase, entry_field, cotangent):
    trans = lax.complex(amplitude * jnp.cos(phase), amplitude * jnp.sin(phase))
    kernel = lax.complex(jnp.cos(kernel_phase), jnp.sin(kernel_phase))
    chi = lax.complex(cotangent[0], cotangent[1])
    grads = [None] * (BLOCKS * SLICE_DEV)
    for block in reversed(range(BLOCKS)):
        field = lax.complex(entry_field[0, block], entry_field[1, block])
        seen = [field]
        for layer in range(SLICE_DEV - 1):
            field = propagate(trans[block * SLICE_DEV + layer] * field, kernel)
            seen.append(field)
        for layer in reversed(range(SLICE_DEV)):
            slot = block * SLICE_DEV + layer
            back = propagate(chi, jnp.conj(kernel))
            grads[slot] = lax.optimization_barrier(jnp.sum(back * jnp.conj(seen[layer]), axis=0)) / math.sqrt(ANGLES)
            chi = back * jnp.conj(trans[slot])
    total = jnp.stack(grads)
    return jnp.stack([jnp.real(total), jnp.imag(total)]).astype(jnp.float32)
```

```python
import functools
import math

import jax
import jax.numpy as jnp
import numpy as np
from jax import lax
from jax.experimental import pallas as pl
from jax.experimental.pallas import tpu as pltpu
from jax.sharding import Mesh, PartitionSpec as P

AXES = ("yh", "z", "x", "yl", "c")
SIZES = (2, 8, 4, 4, 2)
CHIPS = ("yh", "z", "x", "yl")
N = 256
HALF = 128
SLICES = 16
F32 = jnp.float32
BF16 = jnp.bfloat16


def _real_form(angle):
    c, s = np.cos(angle), np.sin(angle)
    return np.block([[c, -s], [s, c]])


def _split_np(m):
    hi = m.astype(BF16)
    return hi, (m - hi.astype(np.float64)).astype(BF16)


@functools.cache
def tables():
    n = np.arange(HALF)
    even = _real_form(2 * np.pi * ((n[:, None] * n[None, :]) % HALF) / HALF)
    odd = _real_form(2 * np.pi * ((n[:, None] * (2 * n[None, :] + 1)) % N) / N)
    core, x, yl, r = np.meshgrid(np.arange(2), np.arange(2), np.arange(4), np.arange(8), indexing="ij")
    order = (x * 64 + yl * 16 + core * 8 + r).reshape(-1)
    both = np.concatenate([order, order + HALF])
    right, left = [], []
    for m in (even, odd, even.T, odd.T):
        hi, lo = _split_np(m)
        right.append(np.stack([hi, lo]))
    for m in (even.T[:, both], odd.T[:, both], even[both, :], odd[both, :]):
        hi, lo = _split_np(m)
        left.append(np.stack([hi, lo]))
    return np.stack(right), np.stack(left)


def prepare_kernel(amp_ref, phase_ref, out_ref):
    amp, phase = amp_ref[0], phase_ref[0]
    re, im = amp * jnp.cos(phase), amp * jnp.sin(phase)
    quarters = (re[:, :HALF], re[:, HALF:], im[:, :HALF], im[:, HALF:])
    for chip in range(256):
        _, z, x, yl = np.unravel_index(chip, SIZES[:4])
        out_ref[chip] = quarters[int(x + 2 * yl + z) % 4]


def prepare(amplitude, phase):
    return pl.pallas_call(
        prepare_kernel,
        out_shape=jax.ShapeDtypeStruct((256, 8, HALF), F32),
        name="prepare",
    )(amplitude, phase)


def split(value):
    hi = value.astype(BF16)
    return hi, (value - hi.astype(F32)).astype(BF16)


def dot_right(value, table):
    hi, lo = split(value)
    wide = jnp.concatenate([table[0], table[0], table[1]], axis=0)
    return jnp.dot(jnp.concatenate([hi, lo, hi], axis=1), wide, preferred_element_type=F32)


def dot_left(table, value):
    hi, lo = split(value)
    wide = jnp.concatenate([table[0], table[0], table[1]], axis=1)
    return jnp.dot(wide, jnp.concatenate([hi, lo, hi], axis=0), preferred_element_type=F32)


def propagate(chi_l, chi_r, right_ref, left_ref, kc_ref, ks_ref):
    ye = dot_right(chi_l + chi_r, right_ref[0])
    yo = dot_right(chi_l - chi_r, right_ref[1])
    re = jnp.concatenate([ye[:, :HALF], yo[:, :HALF]], axis=1)
    im = jnp.concatenate([ye[:, HALF:], yo[:, HALF:]], axis=1)

    def first(v):
        return jnp.concatenate([v[0:64], v[128:192]], axis=0)

    def second(v):
        return jnp.concatenate([v[64:128], v[192:256]], axis=0)

    a = jnp.concatenate([first(re), first(im)], axis=0)
    b = jnp.concatenate([second(re), second(im)], axis=0)
    out = []
    for i, mixed in enumerate((a + b, a - b)):
        freq = dot_left(left_ref[i], mixed)
        fr, fi = freq[:HALF], freq[HALF:]
        c, s = kc_ref[i], ks_ref[i]
        weighted = jnp.concatenate([fr * c + fi * s, fi * c - fr * s], axis=0)
        out.append(dot_left(left_ref[2 + i], weighted))
    top, low = out[0] + out[1], out[0] - out[1]

    def rows(part):
        t, l = top[part * HALF : (part + 1) * HALF], low[part * HALF : (part + 1) * HALF]
        return jnp.concatenate([t[:64], l[:64], t[64:], l[64:]], axis=0)

    re, im = rows(0), rows(1)
    ue = dot_right(jnp.concatenate([re[:, :HALF], im[:, :HALF]], axis=1), right_ref[2])
    uo = dot_right(jnp.concatenate([re[:, HALF:], im[:, HALF:]], axis=1), right_ref[3])
    return ue + uo, ue - uo


def chain_kernel(
    where_ref, cot_ref, psi_ref, kern_ref, right_ref, left_ref, *rest
):
    gathered, (out_ref, t_ref, chi_ref, kc_ref, ks_ref, sem) = rest[:8], rest[8:]
    depth, colour, core = where_ref[0], where_ref[1], where_ref[2]
    other = 1 - core
    near = lax.rem(colour + jnp.where(core == 0, 3, 1), 4)
    far = lax.rem(colour + jnp.where(core == 0, 1, 3), 4)
    across = lax.rem(colour + 2, 4)
    places = (
        (colour, core), (colour, other),
        (near, core), (across, core), (near, other),
        (far, other), (across, other), (far, core),
    )

    def copies(j):
        return [
            pltpu.make_async_copy(ref.at[j], t_ref.at[j, quarter, rows], sem.at[j])
            for ref, (quarter, rows) in zip(gathered, places)
        ]

    def start(i, _):
        for copy in copies(SLICES - 1 - i):
            copy.start()
        return 0

    lax.fori_loop(0, SLICES - 1 - depth, start, 0)

    row = lax.broadcasted_iota(jnp.int32, (N, N), 0)
    col = lax.broadcasted_iota(jnp.int32, (N, N), 1)
    picks = jnp.where(col == jnp.where(row < HALF, 2 * row, 2 * row - (N - 1)), 1.0, 0.0).astype(BF16)
    picks_t = jnp.where(row == jnp.where(col < HALF, 2 * col, 2 * col - (N - 1)), 1.0, 0.0).astype(BF16)

    def three(v):
        hi, rest_ = v.astype(BF16), None
        rest_ = v - hi.astype(F32)
        mid = rest_.astype(BF16)
        return hi, mid, (rest_ - mid.astype(F32)).astype(BF16)

    angle = kern_ref[...]
    angle = sum(jnp.dot(picks, p, preferred_element_type=F32) for p in three(angle))
    angle = sum(jnp.dot(p, picks_t, preferred_element_type=F32) for p in three(angle))
    scale = 1.0 / (N * N)
    kc_ref[...] = (jnp.cos(angle) * scale).reshape(2, HALF, N)
    ks_ref[...] = (jnp.sin(angle) * scale).reshape(2, HALF, N)

    def held(ref, part, half):
        lanes = slice(half * HALF, (half + 1) * HALF)
        return jnp.concatenate([ref[part, :, c, :, lanes].reshape(HALF, HALF) for c in range(2)], axis=0)

    def step(l, r):
        u = propagate(l, r, right_ref, left_ref, kc_ref, ks_ref)
        chi_ref[0], chi_ref[1] = u

    step(*(jnp.concatenate([held(cot_ref, 0, h), held(cot_ref, 1, h)], axis=1) for h in range(2)))

    def body(i, _):
        j = SLICES - 1 - i
        for copy in copies(j):
            copy.wait()
        chi = []
        for h in range(2):
            u = chi_ref[h]
            ur, ui = u[:, :HALF], u[:, HALF:]
            tr = t_ref[j, h].reshape(N, HALF)
            ti = t_ref[j, 2 + h].reshape(N, HALF)
            chi.append(jnp.concatenate([ur * tr + ui * ti, ui * tr - ur * ti], axis=1))
        step(*chi)
        return 0

    lax.fori_loop(0, SLICES - 1 - depth, body, 0)

    for h in range(2):
        lanes = slice(h * HALF, (h + 1) * HALF)
        u = chi_ref[h]
        ur, ui = u[:, :HALF], u[:, HALF:]
        pr, pi = held(psi_ref, 0, h), held(psi_ref, 1, h)
        for part, g in enumerate((ur * pr + ui * pi, ui * pr - ur * pi)):
            for c in range(2):
                out_ref[:, c, part, :, lanes] = g[c * HALF : (c + 1) * HALF].reshape(16, 8, HALF)


def chain(where, cotangent, psi, kernel_phase, gathered):
    right, left = tables()
    vmem = pl.BlockSpec(memory_space=pltpu.VMEM)
    return pl.pallas_call(
        chain_kernel,
        out_shape=jax.ShapeDtypeStruct((16, 2, 2, 8, N), F32),
        in_specs=[pl.BlockSpec(memory_space=pltpu.SMEM)]
        + [vmem] * 5
        + [pl.BlockSpec(memory_space=pl.ANY)] * 8,
        out_specs=vmem,
        scratch_shapes=[
            pltpu.VMEM((SLICES, 4, 2, HALF, HALF), F32),
            pltpu.VMEM((2, N, N), F32),
            pltpu.VMEM((2, HALF, N), F32),
            pltpu.VMEM((2, HALF, N), F32),
            pltpu.SemaphoreType.DMA((SLICES,)),
        ],
        compiler_params=pltpu.CompilerParams(vmem_limit_bytes=40 << 20),
        name="chain",
    )(
        where,
        cotangent.reshape(2, 16, 2, 8, N),
        psi.reshape(2, 16, 2, 8, N),
        kernel_phase,
        jnp.asarray(right),
        jnp.asarray(left),
        *gathered,
    )


def send(value, target):
    pairs = []
    for source in range(int(np.prod(SIZES))):
        yh, z, x, yl, c = (int(v) for v in np.unravel_index(source, SIZES))
        y, z, x, c = target(yh * 4 + yl, z, x, c)
        y %= 8
        pairs.append((source, int(np.ravel_multi_index((y // 4, z % 8, x % 4, y % 4, c), SIZES))))
    return lax.ppermute(value, AXES, pairs)


def per_device(amplitude, phase, kernel_phase, entry_field, cotangent):
    yh, z, x, yl, c = (lax.axis_index(a) for a in AXES)
    where = jnp.stack([yh * 8 + z, lax.rem(x + 2 * yl + z, 4), c]).astype(jnp.int32)
    own = lax.all_to_all(prepare(amplitude, phase), CHIPS, 0, 0).reshape(SLICES, HALF, HALF)
    sign = (1, -1)

    def partner(v):
        return send(v, lambda y, z, x, c: (y, z, x, 1 - c))

    from_x = send(own, lambda y, z, x, c: (y, z, x + sign[c], c))
    from_y = send(own, lambda y, z, x, c: (y + sign[c], z, x, c))
    from_z = send(own, lambda y, z, x, c: (y, z + sign[1 - c], x, 1 - c))
    theirs = partner(own)
    gathered = (own, theirs, from_x, from_y, from_z, partner(from_x), partner(from_y), partner(from_z))
    grad = chain(where, cotangent.reshape(2, N, N), entry_field.reshape(2, N, N), kernel_phase, gathered)
    parts = lax.all_to_all(grad.reshape(32, 2, 8, N), ("x", "yl", "c"), 0, 0)
    return (jnp.sum(parts, axis=0) * (1.0 / math.sqrt(32)))[:, None]


def solution(mesh):
    fine = Mesh(mesh.devices.reshape(SIZES), AXES)
    depth, illum = ("yh", "z"), ("x", "yl", "c")
    return jax.shard_map(
        per_device,
        mesh=fine,
        in_specs=(
            P(depth, illum, None),
            P(depth, illum, None),
            P(),
            P(None, depth, illum, None, None),
            P(None, illum, None, None),
        ),
        out_specs=P(None, depth, illum, None),
        check_vma=False,
    )
```

```python
import functools
import math

import jax
import jax.numpy as jnp
import numpy as np
from jax import lax
from jax.experimental import pallas as pl
from jax.experimental.pallas import tpu as pltpu
from jax.sharding import Mesh, PartitionSpec as P

AXES = ("yh", "z", "x", "yl", "c")
SIZES = (2, 8, 4, 4, 2)
CHIPS = ("yh", "z", "x", "yl")
N = 256
HALF = 128
SLICES = 16
CHUNKS = ((15, 16), (12, 15), (8, 12), (1, 8))
F32 = jnp.float32
BF16 = jnp.bfloat16


def _real_form(angle):
    c, s = np.cos(angle), np.sin(angle)
    return np.block([[c, -s], [s, c]])


def _split_np(m):
    hi = m.astype(BF16)
    return hi, (m - hi.astype(np.float64)).astype(BF16)


@functools.cache
def tables():
    n = np.arange(HALF)
    even = _real_form(2 * np.pi * ((n[:, None] * n[None, :]) % HALF) / HALF)
    odd = _real_form(2 * np.pi * ((n[:, None] * (2 * n[None, :] + 1)) % N) / N)
    core, x, yl, r = np.meshgrid(np.arange(2), np.arange(2), np.arange(4), np.arange(8), indexing="ij")
    order = (x * 64 + yl * 16 + core * 8 + r).reshape(-1)
    both = np.concatenate([order, order + HALF])
    right, left = [], []
    for m in (even, odd, even.T, odd.T):
        hi, lo = _split_np(m)
        right.append(np.stack([hi, lo]))
    for m in (even.T[:, both], odd.T[:, both], even[both, :], odd[both, :]):
        hi, lo = _split_np(m)
        left.append(np.stack([hi, lo]))
    return np.stack(right), np.stack(left)


def prepare_kernel(amp_ref, phase_ref, out_ref):
    amp, phase = amp_ref[0], phase_ref[0]
    re, im = amp * jnp.cos(phase), amp * jnp.sin(phase)
    quarters = (re[:, :HALF], re[:, HALF:], im[:, :HALF], im[:, HALF:])
    for chip in range(256):
        _, z, x, yl = np.unravel_index(chip, SIZES[:4])
        out_ref[chip] = quarters[int(x + 2 * yl + z) % 4]


def prepare(amplitude, phase):
    return pl.pallas_call(
        prepare_kernel,
        out_shape=jax.ShapeDtypeStruct((256, 8, HALF), F32),
        name="prepare",
    )(amplitude, phase)


def split(value):
    hi = value.astype(BF16)
    return hi, (value - hi.astype(F32)).astype(BF16)


def dot_right(value, table):
    hi, lo = split(value)
    wide = jnp.concatenate([table[0], table[0], table[1]], axis=0)
    return jnp.dot(jnp.concatenate([hi, lo, hi], axis=1), wide, preferred_element_type=F32)


def dot_left(table, value):
    hi, lo = split(value)
    wide = jnp.concatenate([table[0], table[0], table[1]], axis=1)
    return jnp.dot(wide, jnp.concatenate([hi, lo, hi], axis=0), preferred_element_type=F32)


def propagate(chi_l, chi_r, right_ref, left_ref, kc_ref, ks_ref):
    ye = dot_right(chi_l + chi_r, right_ref[0])
    yo = dot_right(chi_l - chi_r, right_ref[1])
    re = jnp.concatenate([ye[:, :HALF], yo[:, :HALF]], axis=1)
    im = jnp.concatenate([ye[:, HALF:], yo[:, HALF:]], axis=1)

    def first(v):
        return jnp.concatenate([v[0:64], v[128:192]], axis=0)

    def second(v):
        return jnp.concatenate([v[64:128], v[192:256]], axis=0)

    a = jnp.concatenate([first(re), first(im)], axis=0)
    b = jnp.concatenate([second(re), second(im)], axis=0)
    freqs = [dot_left(left_ref[i], mixed) for i, mixed in enumerate((a + b, a - b))]
    out = []
    for i, freq in enumerate(freqs):
        fr, fi = freq[:HALF], freq[HALF:]
        c, s = kc_ref[i], ks_ref[i]
        weighted = jnp.concatenate([fr * c + fi * s, fi * c - fr * s], axis=0)
        out.append(dot_left(left_ref[2 + i], weighted))
    top, low = out[0] + out[1], out[0] - out[1]

    def rows(part):
        t, l = top[part * HALF : (part + 1) * HALF], low[part * HALF : (part + 1) * HALF]
        return jnp.concatenate([t[:64], l[:64], t[64:], l[64:]], axis=0)

    re, im = rows(0), rows(1)
    ue = dot_right(jnp.concatenate([re[:, :HALF], im[:, :HALF]], axis=1), right_ref[2])
    uo = dot_right(jnp.concatenate([re[:, HALF:], im[:, HALF:]], axis=1), right_ref[3])
    return ue + uo, ue - uo


def three(value):
    hi = value.astype(BF16)
    rest = value - hi.astype(F32)
    mid = rest.astype(BF16)
    return hi, mid, (rest - mid.astype(F32)).astype(BF16)


def held(ref, part, half):
    lanes = slice(half * HALF, (half + 1) * HALF)
    return jnp.concatenate([ref[part, :, c, :, lanes].reshape(HALF, HALF) for c in range(2)], axis=0)


def begin_kernel(order_ref, cot_ref, kern_ref, right_ref, left_ref, u_ref, kc_ref, ks_ref):
    del order_ref
    row = lax.broadcasted_iota(jnp.int32, (N, N), 0)
    col = lax.broadcasted_iota(jnp.int32, (N, N), 1)
    picks = jnp.where(col == jnp.where(row < HALF, 2 * row, 2 * row - (N - 1)), 1.0, 0.0).astype(BF16)
    picks_t = jnp.where(row == jnp.where(col < HALF, 2 * col, 2 * col - (N - 1)), 1.0, 0.0).astype(BF16)
    angle = kern_ref[...]
    angle = sum(jnp.dot(picks, p, preferred_element_type=F32) for p in three(angle))
    angle = sum(jnp.dot(p, picks_t, preferred_element_type=F32) for p in three(angle))
    scale = 1.0 / (N * N)
    kc_ref[...] = (jnp.cos(angle) * scale).reshape(2, HALF, N)
    ks_ref[...] = (jnp.sin(angle) * scale).reshape(2, HALF, N)
    fields = (jnp.concatenate([held(cot_ref, 0, h), held(cot_ref, 1, h)], axis=1) for h in range(2))
    u_ref[0], u_ref[1] = propagate(*fields, right_ref, left_ref, kc_ref, ks_ref)


def chain_kernel(where_ref, u_ref, kc_ref, ks_ref, right_ref, left_ref, psi_hbm, *rest):
    gathered, (own_ref, send_ref, t_ref, chi_ref, psi_ref, sem, psi_sem) = rest[:8], rest[8:]
    depth, colour, core = where_ref[0], where_ref[1], where_ref[2]
    other = 1 - core
    near = lax.rem(colour + jnp.where(core == 0, 3, 1), 4)
    far = lax.rem(colour + jnp.where(core == 0, 1, 3), 4)
    across = lax.rem(colour + 2, 4)
    places = (
        (colour, core), (colour, other),
        (near, core), (across, core), (near, other),
        (far, other), (across, other), (far, core),
    )

    def copies(chunk):
        low, high = CHUNKS[chunk]
        span = slice(low, high)
        return [
            pltpu.make_async_copy(ref.at[span], t_ref.at[quarter, rows, span], sem.at[chunk])
            for ref, (quarter, rows) in zip(gathered, places)
        ]

    for chunk, (_, high) in enumerate(CHUNKS):

        @pl.when(depth < high - 1)
        def _():
            for copy in copies(chunk):
                copy.start()

    psi_copy = pltpu.make_async_copy(psi_hbm, psi_ref, psi_sem)
    psi_copy.start()
    chi_ref[...] = u_ref[...]

    def body(i, _):
        j = SLICES - 1 - i
        for chunk, (_, high) in enumerate(CHUNKS):

            @pl.when(j == high - 1)
            def _():
                for copy in copies(chunk):
                    copy.wait()

        chi = []
        for h in range(2):
            u = chi_ref[h]
            ur, ui = u[:, :HALF], u[:, HALF:]
            tr = t_ref[h, :, j].reshape(N, HALF)
            ti = t_ref[2 + h, :, j].reshape(N, HALF)
            chi.append(jnp.concatenate([ur * tr + ui * ti, ui * tr - ur * ti], axis=1))
        chi_ref[0], chi_ref[1] = propagate(*chi, right_ref, left_ref, kc_ref, ks_ref)
        return 0

    lax.fori_loop(0, SLICES - 1 - depth, body, 0)

    psi_copy.wait()
    for h in range(2):
        lanes = slice(h * HALF, (h + 1) * HALF)
        u = chi_ref[h]
        ur, ui = u[:, :HALF], u[:, HALF:]
        pr, pi = held(psi_ref, 0, h), held(psi_ref, 1, h)
        for part, g in enumerate((ur * pr + ui * pi, ui * pr - ur * pi)):
            first, second = g[:HALF], g[HALF:]
            own_ref[:, part, :, lanes] = jnp.where(core == 0, first, second).reshape(16, 8, HALF)
            send_ref[:, part, :, lanes] = jnp.where(core == 0, second, first).reshape(16, 8, HALF)


VMEM = pl.BlockSpec(memory_space=pltpu.VMEM)
SMEM = pl.BlockSpec(memory_space=pltpu.SMEM)
ANY = pl.BlockSpec(memory_space=pl.ANY)


def begin(order, cotangent, kernel_phase):
    right, left = tables()
    field = jax.ShapeDtypeStruct((2, N, N), F32)
    table = jax.ShapeDtypeStruct((2, HALF, N), F32)
    return pl.pallas_call(
        begin_kernel,
        out_shape=(field, table, table),
        in_specs=[SMEM] + [VMEM] * 4,
        out_specs=(VMEM,) * 3,
        compiler_params=pltpu.CompilerParams(vmem_limit_bytes=24 << 20),
        cost_estimate=pl.CostEstimate(flops=2_000_000_000, bytes_accessed=4 << 20, transcendentals=1 << 17),
        name="begin",
    )(order, cotangent.reshape(2, 16, 2, 8, N), kernel_phase, jnp.asarray(right), jnp.asarray(left))


def chain(where, begun, psi, gathered):
    right, left = tables()
    part = jax.ShapeDtypeStruct((16, 2, 8, N), F32)
    return pl.pallas_call(
        chain_kernel,
        out_shape=(part, part),
        in_specs=[SMEM] + [VMEM] * 5 + [ANY] * 9,
        out_specs=(VMEM, VMEM),
        scratch_shapes=[
            pltpu.VMEM((4, 2, SLICES, HALF, HALF), F32),
            pltpu.VMEM((2, N, N), F32),
            pltpu.VMEM((2, 16, 2, 8, N), F32),
            pltpu.SemaphoreType.DMA((len(CHUNKS),)),
            pltpu.SemaphoreType.DMA,
        ],
        compiler_params=pltpu.CompilerParams(vmem_limit_bytes=40 << 20),
        name="chain",
    )(where, *begun, jnp.asarray(right), jnp.asarray(left), psi.reshape(2, 16, 2, 8, N), *gathered)


def send(value, target):
    pairs = []
    for source in range(int(np.prod(SIZES))):
        yh, z, x, yl, c = (int(v) for v in np.unravel_index(source, SIZES))
        y, z, x, c = target(yh * 4 + yl, z, x, c)
        y %= 8
        pairs.append((source, int(np.ravel_multi_index((y // 4, z % 8, x % 4, y % 4, c), SIZES))))
    return lax.ppermute(value, AXES, pairs)


def per_device(amplitude, phase, kernel_phase, entry_field, cotangent):
    yh, z, x, yl, c = (lax.axis_index(a) for a in AXES)
    where = jnp.stack([yh * 8 + z, lax.rem(x + 2 * yl + z, 4), c]).astype(jnp.int32)
    own = lax.all_to_all(prepare(amplitude, phase), CHIPS, 0, 0).reshape(SLICES, HALF, HALF)
    sign = (1, -1)

    def partner(v):
        return send(v, lambda y, z, x, c: (y, z, x, 1 - c))

    from_x = send(own, lambda y, z, x, c: (y, z, x + sign[c], c))
    from_y = send(own, lambda y, z, x, c: (y + sign[c], z, x, c))
    from_z = send(own, lambda y, z, x, c: (y, z + sign[1 - c], x, 1 - c))
    theirs = partner(own)
    order, _ = lax.optimization_barrier((where, own[:1, :1]))
    begun = begin(order, cotangent.reshape(2, N, N), kernel_phase)
    from_x, begun = lax.optimization_barrier((from_x, begun))
    gathered = (own, theirs, from_x, from_y, from_z, partner(from_x), partner(from_y), partner(from_z))
    mine, others = chain(where, begun, entry_field.reshape(2, N, N), gathered)
    parts = lax.all_to_all(mine + partner(others), ("x", "yl"), 0, 0)
    return (jnp.sum(parts, axis=0) * (1.0 / math.sqrt(32)))[:, None]


def solution(mesh):
    fine = Mesh(mesh.devices.reshape(SIZES), AXES)
    depth, illum = ("yh", "z"), ("x", "yl", "c")
    return jax.shard_map(
        per_device,
        mesh=fine,
        in_specs=(
            P(depth, illum, None),
            P(depth, illum, None),
            P(),
            P(None, depth, illum, None, None),
            P(None, illum, None, None),
        ),
        out_specs=P(None, depth, illum, None),
        check_vma=False,
    )
```

```python
import functools
import math

import jax
import jax.numpy as jnp
import numpy as np
from jax import lax
from jax.experimental import pallas as pl
from jax.experimental.pallas import tpu as pltpu
from jax.sharding import Mesh, PartitionSpec as P

AXES = ("yh", "z", "x", "yl", "c")
SIZES = (2, 8, 4, 4, 2)
N = 256
HALF = 128
SLICES = 16
COLOURS = 4
PEERS = 64
CHUNKS = ((15, 16), (12, 15), (8, 12), (1, 8))
F32 = jnp.float32
BF16 = jnp.bfloat16


def _real_form(angle):
    c, s = np.cos(angle), np.sin(angle)
    return np.block([[c, -s], [s, c]])


def _split_np(m):
    hi = m.astype(BF16)
    return hi, (m - hi.astype(np.float64)).astype(BF16)


@functools.cache
def tables():
    n = np.arange(HALF)
    even = _real_form(2 * np.pi * ((n[:, None] * n[None, :]) % HALF) / HALF)
    odd = _real_form(2 * np.pi * ((n[:, None] * (2 * n[None, :] + 1)) % N) / N)
    core, x, yl, r = np.meshgrid(np.arange(2), np.arange(2), np.arange(4), np.arange(8), indexing="ij")
    order = (x * 64 + yl * 16 + core * 8 + r).reshape(-1)
    both = np.concatenate([order, order + HALF])
    right, left = [], []
    for m in (even, odd, even.T, odd.T):
        hi, lo = _split_np(m)
        right.append(np.stack([hi, lo]))
    for m in (even.T[:, both], odd.T[:, both], even[both, :], odd[both, :]):
        hi, lo = _split_np(m)
        left.append(np.stack([hi, lo]))
    return np.stack(right), np.stack(left)


def sincos(angle):
    turns = jnp.round(angle * (2.0 / math.pi))
    r = ((angle - turns * 1.5703125) - turns * 4.837512969970703125e-4) - turns * 7.54978995489188216e-8
    quadrant = turns.astype(jnp.int32)
    z = r * r
    sine = r + r * z * (-1.6666654611e-1 + z * (8.3321608736e-3 - z * 1.9515295891e-4))
    cosine = 1.0 - 0.5 * z + z * z * (4.166664568298827e-2 + z * (-1.388731625493765e-3 + z * 2.443315711809948e-5))
    odd = (quadrant & 1) == 1
    s, c = jnp.where(odd, cosine, sine), jnp.where(odd, sine, cosine)
    s = jnp.where((quadrant & 2) == 2, -s, s)
    c = jnp.where(((quadrant + 1) & 2) == 2, -c, c)
    return s, c


def prepare_kernel(amp_ref, phase_ref, out_ref):
    amp = amp_ref[0]
    sine, cosine = sincos(phase_ref[0])
    re, im = amp * cosine, amp * sine
    for q, tile in enumerate((re[:, :HALF], re[:, HALF:], im[:, :HALF], im[:, HALF:])):
        for chip in range(PEERS):
            out_ref[chip, q] = tile


def prepare(amplitude, phase):
    return pl.pallas_call(
        prepare_kernel,
        out_shape=jax.ShapeDtypeStruct((PEERS, 4, 8, HALF), F32),
        name="prepare",
    )(amplitude, phase)


def split(value):
    hi = value.astype(BF16)
    return hi, (value - hi.astype(F32)).astype(BF16)


def dot_right(value, table):
    hi, lo = split(value)
    wide = jnp.concatenate([table[0], table[0], table[1]], axis=0)
    return jnp.dot(jnp.concatenate([hi, lo, hi], axis=1), wide, preferred_element_type=F32)


def dot_left(table, value):
    hi, lo = split(value)
    wide = jnp.concatenate([table[0], table[0], table[1]], axis=1)
    return jnp.dot(wide, jnp.concatenate([hi, lo, hi], axis=0), preferred_element_type=F32)


def propagate(chi_l, chi_r, right_ref, left_ref, kc_ref, ks_ref):
    ye = dot_right(chi_l + chi_r, right_ref[0])
    yo = dot_right(chi_l - chi_r, right_ref[1])
    re = jnp.concatenate([ye[:, :HALF], yo[:, :HALF]], axis=1)
    im = jnp.concatenate([ye[:, HALF:], yo[:, HALF:]], axis=1)

    def first(v):
        return jnp.concatenate([v[0:64], v[128:192]], axis=0)

    def second(v):
        return jnp.concatenate([v[64:128], v[192:256]], axis=0)

    a = jnp.concatenate([first(re), first(im)], axis=0)
    b = jnp.concatenate([second(re), second(im)], axis=0)
    freqs = [dot_left(left_ref[i], mixed) for i, mixed in enumerate((a + b, a - b))]
    out = []
    for i, freq in enumerate(freqs):
        fr, fi = freq[:HALF], freq[HALF:]
        c, s = kc_ref[i], ks_ref[i]
        weighted = jnp.concatenate([fr * c + fi * s, fi * c - fr * s], axis=0)
        out.append(dot_left(left_ref[2 + i], weighted))
    top, low = out[0] + out[1], out[0] - out[1]

    def rows(part):
        t, l = top[part * HALF : (part + 1) * HALF], low[part * HALF : (part + 1) * HALF]
        return jnp.concatenate([t[:64], l[:64], t[64:], l[64:]], axis=0)

    re, im = rows(0), rows(1)
    ue = dot_right(jnp.concatenate([re[:, :HALF], im[:, :HALF]], axis=1), right_ref[2])
    uo = dot_right(jnp.concatenate([re[:, HALF:], im[:, HALF:]], axis=1), right_ref[3])
    return ue + uo, ue - uo


def three(value):
    hi = value.astype(BF16)
    rest = value - hi.astype(F32)
    mid = rest.astype(BF16)
    return hi, mid, (rest - mid.astype(F32)).astype(BF16)


def held(ref, part, half):
    lanes = slice(half * HALF, (half + 1) * HALF)
    return jnp.concatenate([ref[part, :, c, :, lanes].reshape(HALF, HALF) for c in range(2)], axis=0)


def begin_kernel(order_ref, cot_ref, kern_ref, right_ref, left_ref, u_ref, kc_ref, ks_ref):
    del order_ref
    row = lax.broadcasted_iota(jnp.int32, (N, N), 0)
    col = lax.broadcasted_iota(jnp.int32, (N, N), 1)
    picks = jnp.where(col == jnp.where(row < HALF, 2 * row, 2 * row - (N - 1)), 1.0, 0.0).astype(BF16)
    picks_t = jnp.where(row == jnp.where(col < HALF, 2 * col, 2 * col - (N - 1)), 1.0, 0.0).astype(BF16)
    angle = kern_ref[...]
    angle = sum(jnp.dot(picks, p, preferred_element_type=F32) for p in three(angle))
    angle = sum(jnp.dot(p, picks_t, preferred_element_type=F32) for p in three(angle))
    scale = 1.0 / (N * N)
    sine, cosine = sincos(angle)
    kc_ref[...] = (cosine * scale).reshape(2, HALF, N)
    ks_ref[...] = (sine * scale).reshape(2, HALF, N)
    fields = (jnp.concatenate([held(cot_ref, 0, h), held(cot_ref, 1, h)], axis=1) for h in range(2))
    u_ref[0], u_ref[1] = propagate(*fields, right_ref, left_ref, kc_ref, ks_ref)


def chain_kernel(where_ref, u_ref, kc_ref, ks_ref, right_ref, left_ref, psi_hbm, *rest):
    gathered, (own_ref, send_ref, t_ref, chi_ref, psi_ref, sem, psi_sem) = rest[:8], rest[8:]
    depth, colour, core = where_ref[0], where_ref[1], where_ref[2]
    other = 1 - core
    near = lax.rem(colour + jnp.where(core == 0, 3, 1), 4)
    far = lax.rem(colour + jnp.where(core == 0, 1, 3), 4)
    across = lax.rem(colour + 2, 4)
    places = (
        (colour, core), (colour, other),
        (near, core), (across, core), (near, other),
        (far, other), (across, other), (far, core),
    )

    def copies(chunk):
        low, high = CHUNKS[chunk]
        span = slice(low, high)
        return [
            pltpu.make_async_copy(ref.at[span], t_ref.at[hue, rows, span], sem.at[chunk])
            for ref, (hue, rows) in zip(gathered, places)
        ]

    for chunk, (_, high) in enumerate(CHUNKS):

        @pl.when(depth < high - 1)
        def _():
            for copy in copies(chunk):
                copy.start()

    psi_copy = pltpu.make_async_copy(psi_hbm, psi_ref, psi_sem)
    psi_copy.start()
    chi_ref[...] = u_ref[...]

    def body(i, _):
        j = SLICES - 1 - i
        for chunk, (_, high) in enumerate(CHUNKS):

            @pl.when(j == high - 1)
            def _():
                for copy in copies(chunk):
                    copy.wait()

        hues = [(j + e) & 3 for e in range(COLOURS)]

        def rows_of(q):
            tiles = [
                t_ref[hues[(x + 2 * yl) & 3], c, j, yl, q] for c in range(2) for x in range(4) for yl in range(4)
            ]
            return jnp.concatenate(tiles, axis=0)

        chi = []
        for h in range(2):
            u = chi_ref[h]
            ur, ui = u[:, :HALF], u[:, HALF:]
            tr, ti = rows_of(h), rows_of(2 + h)
            chi.append(jnp.concatenate([ur * tr + ui * ti, ui * tr - ur * ti], axis=1))
        chi_ref[0], chi_ref[1] = propagate(*chi, right_ref, left_ref, kc_ref, ks_ref)
        return 0

    lax.fori_loop(0, SLICES - 1 - depth, body, 0)

    psi_copy.wait()
    for h in range(2):
        lanes = slice(h * HALF, (h + 1) * HALF)
        u = chi_ref[h]
        ur, ui = u[:, :HALF], u[:, HALF:]
        pr, pi = held(psi_ref, 0, h), held(psi_ref, 1, h)
        for part, g in enumerate((ur * pr + ui * pi, ui * pr - ur * pi)):
            first, second = g[:HALF], g[HALF:]
            own_ref[:, part, :, lanes] = jnp.where(core == 0, first, second).reshape(16, 8, HALF)
            send_ref[:, part, :, lanes] = jnp.where(core == 0, second, first).reshape(16, 8, HALF)


VMEM = pl.BlockSpec(memory_space=pltpu.VMEM)
SMEM = pl.BlockSpec(memory_space=pltpu.SMEM)
ANY = pl.BlockSpec(memory_space=pl.ANY)


def begin(order, cotangent, kernel_phase):
    right, left = tables()
    field = jax.ShapeDtypeStruct((2, N, N), F32)
    table = jax.ShapeDtypeStruct((2, HALF, N), F32)
    return pl.pallas_call(
        begin_kernel,
        out_shape=(field, table, table),
        in_specs=[SMEM] + [VMEM] * 4,
        out_specs=(VMEM,) * 3,
        compiler_params=pltpu.CompilerParams(vmem_limit_bytes=24 << 20),
        cost_estimate=pl.CostEstimate(flops=2_000_000_000, bytes_accessed=4 << 20, transcendentals=1 << 17),
        name="begin",
    )(order, cotangent.reshape(2, 16, 2, 8, N), kernel_phase, jnp.asarray(right), jnp.asarray(left))


def chain(where, begun, psi, gathered):
    right, left = tables()
    part = jax.ShapeDtypeStruct((16, 2, 8, N), F32)
    return pl.pallas_call(
        chain_kernel,
        out_shape=(part, part),
        in_specs=[SMEM] + [VMEM] * 5 + [ANY] * 9,
        out_specs=(VMEM, VMEM),
        scratch_shapes=[
            pltpu.VMEM((COLOURS, 2, SLICES, 4, 4, 8, HALF), F32),
            pltpu.VMEM((2, N, N), F32),
            pltpu.VMEM((2, 16, 2, 8, N), F32),
            pltpu.SemaphoreType.DMA((len(CHUNKS),)),
            pltpu.SemaphoreType.DMA,
        ],
        compiler_params=pltpu.CompilerParams(vmem_limit_bytes=22 << 20),
        name="chain",
    )(where, *begun, jnp.asarray(right), jnp.asarray(left), psi.reshape(2, 16, 2, 8, N), *gathered)


def send(value, target):
    pairs = []
    for source in range(int(np.prod(SIZES))):
        yh, z, x, yl, c = (int(v) for v in np.unravel_index(source, SIZES))
        y, z, x, c = target(yh * 4 + yl, z, x, c)
        y %= 8
        pairs.append((source, int(np.ravel_multi_index((y // 4, z % 8, x % 4, y % 4, c), SIZES))))
    return lax.ppermute(value, AXES, pairs)


def colour_groups():
    groups = {}
    for yh, z, yl, x, c in np.ndindex(2, 8, 4, 4, 2):
        device = int(np.ravel_multi_index((yh, z, x, yl, c), SIZES))
        groups.setdefault(((x + 2 * yl + z) % COLOURS, c), []).append(device)
    return [groups[key] for key in sorted(groups)]


def per_device(amplitude, phase, kernel_phase, entry_field, cotangent):
    yh, z, x, yl, c = (lax.axis_index(a) for a in AXES)
    where = jnp.stack([yh * 8 + z, lax.rem(x + 2 * yl + z, 4), c]).astype(jnp.int32)
    own = lax.all_to_all(prepare(amplitude, phase), AXES, 0, 0, axis_index_groups=colour_groups())
    own = own.reshape(SLICES, 4, 4, 8, HALF)
    sign = (1, -1)

    def partner(v):
        return send(v, lambda y, z, x, c: (y, z, x, 1 - c))

    from_x = send(own, lambda y, z, x, c: (y, z, x + sign[c], c))
    from_y = send(own, lambda y, z, x, c: (y + sign[c], z, x, c))
    from_z = send(own, lambda y, z, x, c: (y, z + sign[1 - c], x, 1 - c))
    theirs = partner(own)
    order, _ = lax.optimization_barrier((where, own[:1, :1, :1]))
    begun = begin(order, cotangent.reshape(2, N, N), kernel_phase)
    from_x, begun = lax.optimization_barrier((from_x, begun))
    gathered = (own, theirs, from_x, from_y, from_z, partner(from_x), partner(from_y), partner(from_z))
    mine, others = chain(where, begun, entry_field.reshape(2, N, N), gathered)
    parts = lax.all_to_all(mine + partner(others), ("x", "yl"), 0, 0)
    return (jnp.sum(parts, axis=0) * (1.0 / math.sqrt(32)))[:, None]


def solution(mesh):
    fine = Mesh(mesh.devices.reshape(SIZES), AXES)
    depth, illum = ("yh", "z"), ("x", "yl", "c")
    return jax.shard_map(
        per_device,
        mesh=fine,
        in_specs=(
            P(depth, illum, None),
            P(depth, illum, None),
            P(),
            P(None, depth, illum, None, None),
            P(None, illum, None, None),
        ),
        out_specs=P(None, depth, illum, None),
        check_vma=False,
    )
```

```python
import functools
import math

import jax
import jax.numpy as jnp
import numpy as np
from jax import lax
from jax.experimental import pallas as pl
from jax.experimental.pallas import tpu as pltpu
from jax.sharding import Mesh, PartitionSpec as P

AXES = ("yh", "z", "x", "yl", "c")
SIZES = (2, 8, 4, 4, 2)
N = 256
HALF = 128
SLICES = 16
COLOURS = 4
PEERS = 64
CHUNKS = ((1, SLICES),)
F32 = jnp.float32
BF16 = jnp.bfloat16


def _real_form(angle):
    c, s = np.cos(angle), np.sin(angle)
    return np.block([[c, -s], [s, c]])


def _split_np(m):
    hi = m.astype(BF16)
    return hi, (m - hi.astype(np.float64)).astype(BF16)


@functools.cache
def tables():
    n = np.arange(HALF)
    even = _real_form(2 * np.pi * ((n[:, None] * n[None, :]) % HALF) / HALF)
    odd = _real_form(2 * np.pi * ((n[:, None] * (2 * n[None, :] + 1)) % N) / N)
    core, x, yl, r = np.meshgrid(np.arange(2), np.arange(2), np.arange(4), np.arange(8), indexing="ij")
    order = (x * 64 + yl * 16 + core * 8 + r).reshape(-1)
    both = np.concatenate([order, order + HALF])
    right, left = [], []
    for m in (even, odd, even.T, odd.T):
        hi, lo = _split_np(m)
        right.append(np.stack([hi, lo]))
    for m in (even.T[:, both], odd.T[:, both], even[both, :], odd[both, :]):
        hi, lo = _split_np(m)
        left.append(np.stack([hi, lo]))
    return np.stack(right), np.stack(left)


def sincos(angle):
    turns = jnp.round(angle * (2.0 / math.pi))
    r = ((angle - turns * 1.5703125) - turns * 4.837512969970703125e-4) - turns * 7.54978995489188216e-8
    quadrant = turns.astype(jnp.int32)
    z = r * r
    sine = r + r * z * (-1.6666654611e-1 + z * (8.3321608736e-3 - z * 1.9515295891e-4))
    cosine = 1.0 - 0.5 * z + z * z * (4.166664568298827e-2 + z * (-1.388731625493765e-3 + z * 2.443315711809948e-5))
    odd = (quadrant & 1) == 1
    s, c = jnp.where(odd, cosine, sine), jnp.where(odd, sine, cosine)
    s = jnp.where((quadrant & 2) == 2, -s, s)
    c = jnp.where(((quadrant + 1) & 2) == 2, -c, c)
    return s, c


def prepare_kernel(amp_ref, phase_ref, out_ref):
    amp = amp_ref[0]
    sine, cosine = sincos(phase_ref[0])
    re, im = amp * cosine, amp * sine
    for q, tile in enumerate((re[:, :HALF], re[:, HALF:], im[:, :HALF], im[:, HALF:])):
        for chip in range(PEERS):
            out_ref[chip, q] = tile


def prepare(amplitude, phase):
    return pl.pallas_call(
        prepare_kernel,
        out_shape=pltpu.VMEM((PEERS, 4, 8, HALF), F32),
        name="prepare",
    )(amplitude, phase)


def split(value):
    hi = value.astype(BF16)
    return hi, (value - hi.astype(F32)).astype(BF16)


def dot_right(value, table):
    hi, lo = split(value)
    wide = jnp.concatenate([table[0], table[0], table[1]], axis=0)
    return jnp.dot(jnp.concatenate([hi, lo, hi], axis=1), wide, preferred_element_type=F32)


def dot_left(table, value):
    hi, lo = split(value)
    wide = jnp.concatenate([table[0], table[0], table[1]], axis=1)
    return jnp.dot(wide, jnp.concatenate([hi, lo, hi], axis=0), preferred_element_type=F32)


def propagate(chi_l, chi_r, right_ref, left_ref, kc_ref, ks_ref):
    ye = dot_right(chi_l + chi_r, right_ref[0])
    yo = dot_right(chi_l - chi_r, right_ref[1])
    re = jnp.concatenate([ye[:, :HALF], yo[:, :HALF]], axis=1)
    im = jnp.concatenate([ye[:, HALF:], yo[:, HALF:]], axis=1)

    def first(v):
        return jnp.concatenate([v[0:64], v[128:192]], axis=0)

    def second(v):
        return jnp.concatenate([v[64:128], v[192:256]], axis=0)

    a = jnp.concatenate([first(re), first(im)], axis=0)
    b = jnp.concatenate([second(re), second(im)], axis=0)
    freqs = [dot_left(left_ref[i], mixed) for i, mixed in enumerate((a + b, a - b))]
    out = []
    for i, freq in enumerate(freqs):
        fr, fi = freq[:HALF], freq[HALF:]
        c, s = kc_ref[i], ks_ref[i]
        weighted = jnp.concatenate([fr * c + fi * s, fi * c - fr * s], axis=0)
        out.append(dot_left(left_ref[2 + i], weighted))
    top, low = out[0] + out[1], out[0] - out[1]

    def rows(part):
        t, l = top[part * HALF : (part + 1) * HALF], low[part * HALF : (part + 1) * HALF]
        return jnp.concatenate([t[:64], l[:64], t[64:], l[64:]], axis=0)

    re, im = rows(0), rows(1)
    ue = dot_right(jnp.concatenate([re[:, :HALF], im[:, :HALF]], axis=1), right_ref[2])
    uo = dot_right(jnp.concatenate([re[:, HALF:], im[:, HALF:]], axis=1), right_ref[3])
    return ue + uo, ue - uo


def three(value):
    hi = value.astype(BF16)
    rest = value - hi.astype(F32)
    mid = rest.astype(BF16)
    return hi, mid, (rest - mid.astype(F32)).astype(BF16)


def held(ref, part, half):
    lanes = slice(half * HALF, (half + 1) * HALF)
    return jnp.concatenate([ref[part, :, c, :, lanes].reshape(HALF, HALF) for c in range(2)], axis=0)


def begin_kernel(order_ref, cot_ref, kern_ref, right_ref, left_ref, u_ref, kc_ref, ks_ref):
    del order_ref
    row = lax.broadcasted_iota(jnp.int32, (N, N), 0)
    col = lax.broadcasted_iota(jnp.int32, (N, N), 1)
    picks = jnp.where(col == jnp.where(row < HALF, 2 * row, 2 * row - (N - 1)), 1.0, 0.0).astype(BF16)
    picks_t = jnp.where(row == jnp.where(col < HALF, 2 * col, 2 * col - (N - 1)), 1.0, 0.0).astype(BF16)
    angle = kern_ref[...]
    angle = sum(jnp.dot(picks, p, preferred_element_type=F32) for p in three(angle))
    angle = sum(jnp.dot(p, picks_t, preferred_element_type=F32) for p in three(angle))
    scale = 1.0 / (N * N)
    sine, cosine = sincos(angle)
    kc_ref[...] = (cosine * scale).reshape(2, HALF, N)
    ks_ref[...] = (sine * scale).reshape(2, HALF, N)
    fields = (jnp.concatenate([held(cot_ref, 0, h), held(cot_ref, 1, h)], axis=1) for h in range(2))
    u_ref[0], u_ref[1] = propagate(*fields, right_ref, left_ref, kc_ref, ks_ref)


def chain_kernel(where_ref, u_ref, kc_ref, ks_ref, right_ref, left_ref, psi_hbm, *rest):
    gathered, (own_ref, send_ref, t_ref, chi_ref, psi_ref, sem, psi_sem) = rest[:8], rest[8:]
    depth, colour, core = where_ref[0], where_ref[1], where_ref[2]
    other = 1 - core
    near = lax.rem(colour + jnp.where(core == 0, 3, 1), 4)
    far = lax.rem(colour + jnp.where(core == 0, 1, 3), 4)
    across = lax.rem(colour + 2, 4)
    places = (
        (colour, core), (colour, other),
        (near, core), (across, core), (near, other),
        (far, other), (across, other), (far, core),
    )

    def copies(chunk):
        low, high = CHUNKS[chunk]
        span = slice(low, high)
        return [
            pltpu.make_async_copy(ref.at[span], t_ref.at[hue, rows, span], sem.at[chunk])
            for ref, (hue, rows) in zip(gathered, places)
        ]

    for chunk, (_, high) in enumerate(CHUNKS):

        @pl.when(depth < high - 1)
        def _():
            for copy in copies(chunk):
                copy.start()

    psi_copy = pltpu.make_async_copy(psi_hbm, psi_ref, psi_sem)
    psi_copy.start()
    chi_ref[...] = u_ref[...]

    def body(i, _):
        j = SLICES - 1 - i
        for chunk, (_, high) in enumerate(CHUNKS):

            @pl.when(j == high - 1)
            def _():
                for copy in copies(chunk):
                    copy.wait()

        hues = [(j + e) & 3 for e in range(COLOURS)]

        def rows_of(q):
            tiles = [
                t_ref[hues[(x + 2 * yl) & 3], c, j, yl, q] for c in range(2) for x in range(4) for yl in range(4)
            ]
            return jnp.concatenate(tiles, axis=0)

        chi = []
        for h in range(2):
            u = chi_ref[h]
            ur, ui = u[:, :HALF], u[:, HALF:]
            tr, ti = rows_of(h), rows_of(2 + h)
            chi.append(jnp.concatenate([ur * tr + ui * ti, ui * tr - ur * ti], axis=1))
        chi_ref[0], chi_ref[1] = propagate(*chi, right_ref, left_ref, kc_ref, ks_ref)
        return 0

    lax.fori_loop(0, SLICES - 1 - depth, body, 0)

    psi_copy.wait()
    for h in range(2):
        lanes = slice(h * HALF, (h + 1) * HALF)
        u = chi_ref[h]
        ur, ui = u[:, :HALF], u[:, HALF:]
        pr, pi = held(psi_ref, 0, h), held(psi_ref, 1, h)
        for part, g in enumerate((ur * pr + ui * pi, ui * pr - ur * pi)):
            first, second = g[:HALF], g[HALF:]
            own_ref[:, part, :, lanes] = jnp.where(core == 0, first, second).reshape(16, 8, HALF)
            send_ref[:, part, :, lanes] = jnp.where(core == 0, second, first).reshape(16, 8, HALF)


VMEM = pl.BlockSpec(memory_space=pltpu.VMEM)
SMEM = pl.BlockSpec(memory_space=pltpu.SMEM)
ANY = pl.BlockSpec(memory_space=pl.ANY)


def begin(order, cotangent, kernel_phase):
    right, left = tables()
    field = jax.ShapeDtypeStruct((2, N, N), F32)
    table = jax.ShapeDtypeStruct((2, HALF, N), F32)
    return pl.pallas_call(
        begin_kernel,
        out_shape=(field, table, table),
        in_specs=[SMEM] + [VMEM] * 4,
        out_specs=(VMEM,) * 3,
        compiler_params=pltpu.CompilerParams(vmem_limit_bytes=24 << 20),
        cost_estimate=pl.CostEstimate(flops=2_000_000_000, bytes_accessed=4 << 20, transcendentals=1 << 17),
        name="begin",
    )(order, cotangent.reshape(2, 16, 2, 8, N), kernel_phase, jnp.asarray(right), jnp.asarray(left))


def chain(where, begun, psi, gathered):
    right, left = tables()
    part = jax.ShapeDtypeStruct((16, 2, 8, N), F32)
    return pl.pallas_call(
        chain_kernel,
        out_shape=(part, part),
        in_specs=[SMEM] + [VMEM] * 5 + [ANY] * 9,
        out_specs=(VMEM, VMEM),
        scratch_shapes=[
            pltpu.VMEM((COLOURS, 2, SLICES, 4, 4, 8, HALF), F32),
            pltpu.VMEM((2, N, N), F32),
            pltpu.VMEM((2, 16, 2, 8, N), F32),
            pltpu.SemaphoreType.DMA((len(CHUNKS),)),
            pltpu.SemaphoreType.DMA,
        ],
        compiler_params=pltpu.CompilerParams(vmem_limit_bytes=22 << 20),
        name="chain",
    )(where, *begun, jnp.asarray(right), jnp.asarray(left), psi.reshape(2, 16, 2, 8, N), *gathered)


def send(value, target):
    pairs = []
    for source in range(int(np.prod(SIZES))):
        yh, z, x, yl, c = (int(v) for v in np.unravel_index(source, SIZES))
        y, z, x, c = target(yh * 4 + yl, z, x, c)
        y %= 8
        pairs.append((source, int(np.ravel_multi_index((y // 4, z % 8, x % 4, y % 4, c), SIZES))))
    return lax.ppermute(value, AXES, pairs)


def colour_groups():
    groups = {}
    for yh, z, yl, x, c in np.ndindex(2, 8, 4, 4, 2):
        device = int(np.ravel_multi_index((yh, z, x, yl, c), SIZES))
        groups.setdefault(((x + 2 * yl + z) % COLOURS, c), []).append(device)
    return [groups[key] for key in sorted(groups)]


def per_device(amplitude, phase, kernel_phase, entry_field, cotangent):
    yh, z, x, yl, c = (lax.axis_index(a) for a in AXES)
    where = jnp.stack([yh * 8 + z, lax.rem(x + 2 * yl + z, 4), c]).astype(jnp.int32)
    own = lax.all_to_all(prepare(amplitude, phase), AXES, 0, 0, axis_index_groups=colour_groups())
    own = own.reshape(SLICES, 4, 4, 8, HALF)
    sign = (1, -1)

    def partner(v):
        return send(v, lambda y, z, x, c: (y, z, x, 1 - c))

    from_x = send(own, lambda y, z, x, c: (y, z, x + sign[c], c))
    from_y = send(own, lambda y, z, x, c: (y + sign[c], z, x, c))
    from_z = send(own, lambda y, z, x, c: (y, z + sign[1 - c], x, 1 - c))
    theirs = partner(own)
    order, _ = lax.optimization_barrier((where, own[:1, :1, :1]))
    begun = begin(order, cotangent.reshape(2, N, N), kernel_phase)
    from_x, begun = lax.optimization_barrier((from_x, begun))
    their_x = partner(from_x)
    their_y = partner(from_y)
    their_z = partner(from_z)
    gathered = (own, theirs, from_x, from_y, from_z, their_x, their_y, their_z)
    mine, others = chain(where, begun, entry_field.reshape(2, N, N), gathered)
    parts = lax.all_to_all(mine + partner(others), ("x", "yl"), 0, 0)
    return (jnp.sum(parts, axis=0) * (1.0 / math.sqrt(32)))[:, None]


def solution(mesh):
    fine = Mesh(mesh.devices.reshape(SIZES), AXES)
    depth, illum = ("yh", "z"), ("x", "yl", "c")
    return jax.shard_map(
        per_device,
        mesh=fine,
        in_specs=(
            P(depth, illum, None),
            P(depth, illum, None),
            P(),
            P(None, depth, illum, None, None),
            P(None, illum, None, None),
        ),
        out_specs=P(None, depth, illum, None),
        check_vma=False,
    )
```

```python
import functools
import math

import jax
import jax.numpy as jnp
import numpy as np
from jax import lax
from jax.experimental import pallas as pl
from jax.experimental.pallas import tpu as pltpu
from jax.sharding import Mesh, PartitionSpec as P

AXES = ("yh", "z", "x", "yl", "c")
SIZES = (2, 8, 4, 4, 2)
N = 256
HALF = 128
SLICES = 16
COLOURS = 4
PEERS = 64
EARLY = 5
F32 = jnp.float32
BF16 = jnp.bfloat16


def _real_form(angle):
    c, s = np.cos(angle), np.sin(angle)
    return np.block([[c, -s], [s, c]])


def _split_np(m):
    hi = m.astype(BF16)
    return hi, (m - hi.astype(np.float64)).astype(BF16)


@functools.cache
def tables():
    n = np.arange(HALF)
    even = _real_form(2 * np.pi * ((n[:, None] * n[None, :]) % HALF) / HALF)
    odd = _real_form(2 * np.pi * ((n[:, None] * (2 * n[None, :] + 1)) % N) / N)
    core, x, yl, r = np.meshgrid(np.arange(2), np.arange(2), np.arange(4), np.arange(8), indexing="ij")
    order = (x * 64 + yl * 16 + core * 8 + r).reshape(-1)
    both = np.concatenate([order, order + HALF])
    right, left = [], []
    for m in (even, odd, even.T, odd.T):
        hi, lo = _split_np(m)
        right.append(np.stack([hi, lo]))
    for m in (even.T[:, both], odd.T[:, both], even[both, :], odd[both, :]):
        hi, lo = _split_np(m)
        left.append(np.stack([hi, lo]))
    return np.stack(right + left)


def sincos(angle):
    turns = jnp.round(angle * (2.0 / math.pi))
    r = ((angle - turns * 1.5703125) - turns * 4.837512969970703125e-4) - turns * 7.54978995489188216e-8
    quadrant = turns.astype(jnp.int32)
    z = r * r
    sine = r + r * z * (-1.6666654611e-1 + z * (8.3321608736e-3 - z * 1.9515295891e-4))
    cosine = 1.0 - 0.5 * z + z * z * (4.166664568298827e-2 + z * (-1.388731625493765e-3 + z * 2.443315711809948e-5))
    odd = (quadrant & 1) == 1
    s, c = jnp.where(odd, cosine, sine), jnp.where(odd, sine, cosine)
    s = jnp.where((quadrant & 2) == 2, -s, s)
    c = jnp.where(((quadrant + 1) & 2) == 2, -c, c)
    return s, c


def prepare_kernel(amp_ref, phase_ref, out_ref):
    amp = amp_ref[0]
    sine, cosine = sincos(phase_ref[0])
    re, im = amp * cosine, amp * sine
    for q, tile in enumerate((re[:, :HALF], re[:, HALF:], im[:, :HALF], im[:, HALF:])):
        for chip in range(PEERS):
            out_ref[chip, q] = tile


def prepare(amplitude, phase):
    return pl.pallas_call(
        prepare_kernel,
        out_shape=pltpu.VMEM((PEERS, 4, 8, HALF), F32),
        name="prepare",
    )(amplitude, phase)


def split(value):
    hi = value.astype(BF16)
    return hi, (value - hi.astype(F32)).astype(BF16)


def dot_right(value, table):
    hi, lo = split(value)
    wide = jnp.concatenate([table[0], table[0], table[1]], axis=0)
    return jnp.dot(jnp.concatenate([hi, lo, hi], axis=1), wide, preferred_element_type=F32)


def dot_left(table, value):
    hi, lo = split(value)
    wide = jnp.concatenate([table[0], table[0], table[1]], axis=1)
    return jnp.dot(wide, jnp.concatenate([hi, lo, hi], axis=0), preferred_element_type=F32)


def propagate(chi_l, chi_r, table_ref, kc_ref, ks_ref):
    ye = dot_right(chi_l + chi_r, table_ref[0])
    yo = dot_right(chi_l - chi_r, table_ref[1])
    re = jnp.concatenate([ye[:, :HALF], yo[:, :HALF]], axis=1)
    im = jnp.concatenate([ye[:, HALF:], yo[:, HALF:]], axis=1)

    def first(v):
        return jnp.concatenate([v[0:64], v[128:192]], axis=0)

    def second(v):
        return jnp.concatenate([v[64:128], v[192:256]], axis=0)

    a = jnp.concatenate([first(re), first(im)], axis=0)
    b = jnp.concatenate([second(re), second(im)], axis=0)
    freqs = [dot_left(table_ref[4 + i], mixed) for i, mixed in enumerate((a + b, a - b))]
    out = []
    for i, freq in enumerate(freqs):
        fr, fi = freq[:HALF], freq[HALF:]
        c, s = kc_ref[i], ks_ref[i]
        weighted = jnp.concatenate([fr * c + fi * s, fi * c - fr * s], axis=0)
        out.append(dot_left(table_ref[6 + i], weighted))
    top, low = out[0] + out[1], out[0] - out[1]

    def rows(part):
        t, l = top[part * HALF : (part + 1) * HALF], low[part * HALF : (part + 1) * HALF]
        return jnp.concatenate([t[:64], l[:64], t[64:], l[64:]], axis=0)

    re, im = rows(0), rows(1)
    ue = dot_right(jnp.concatenate([re[:, :HALF], im[:, :HALF]], axis=1), table_ref[2])
    uo = dot_right(jnp.concatenate([re[:, HALF:], im[:, HALF:]], axis=1), table_ref[3])
    return ue + uo, ue - uo


def three(value):
    hi = value.astype(BF16)
    rest = value - hi.astype(F32)
    mid = rest.astype(BF16)
    return hi, mid, (rest - mid.astype(F32)).astype(BF16)


def held(ref, part, half):
    lanes = slice(half * HALF, (half + 1) * HALF)
    return jnp.concatenate([ref[part, :, c, :, lanes].reshape(HALF, HALF) for c in range(2)], axis=0)


def begin_kernel(order_ref, cot_ref, kern_ref, table_ref, u_ref, kc_ref, ks_ref):
    del order_ref
    row = lax.broadcasted_iota(jnp.int32, (N, N), 0)
    col = lax.broadcasted_iota(jnp.int32, (N, N), 1)
    picks = jnp.where(col == jnp.where(row < HALF, 2 * row, 2 * row - (N - 1)), 1.0, 0.0).astype(BF16)
    picks_t = jnp.where(row == jnp.where(col < HALF, 2 * col, 2 * col - (N - 1)), 1.0, 0.0).astype(BF16)
    angle = kern_ref[...]
    angle = sum(jnp.dot(picks, p, preferred_element_type=F32) for p in three(angle))
    angle = sum(jnp.dot(p, picks_t, preferred_element_type=F32) for p in three(angle))
    scale = 1.0 / (N * N)
    sine, cosine = sincos(angle)
    kc_ref[...] = (cosine * scale).reshape(2, HALF, N)
    ks_ref[...] = (sine * scale).reshape(2, HALF, N)
    fields = (jnp.concatenate([held(cot_ref, 0, h), held(cot_ref, 1, h)], axis=1) for h in range(2))
    u_ref[0], u_ref[1] = propagate(*fields, table_ref, kc_ref, ks_ref)


def places(where_ref):
    colour, core = where_ref[1], where_ref[2]
    other = 1 - core
    near = lax.rem(colour + jnp.where(core == 0, 3, 1), COLOURS)
    far = lax.rem(colour + jnp.where(core == 0, 1, 3), COLOURS)
    across = lax.rem(colour + 2, COLOURS)
    return (
        (colour, core), (colour, other),
        (near, core), (across, core), (near, other),
        (far, other), (across, other), (far, core),
    )


def placing(arrays, slots, t_ref, sem):
    used = slice(1, SLICES)
    return [
        pltpu.make_async_copy(ref.at[used], t_ref.at[hue, rows, used], sem)
        for ref, (hue, rows) in zip(arrays, slots)
    ]


def place_kernel(where_ref, *rest):
    arrays, (t_ref, sem) = rest[:EARLY], rest[EARLY:]
    copies = placing(arrays, places(where_ref)[:EARLY], t_ref, sem)
    for copy in copies:
        copy.start()
    for copy in copies:
        copy.wait()


def chain_kernel(where_ref, u_ref, kc_ref, ks_ref, table_ref, psi_hbm, placed_ref, *rest):
    del placed_ref
    late, (own_ref, send_ref, t_ref, chi_ref, psi_ref, sem, psi_sem) = rest[: 8 - EARLY], rest[8 - EARLY :]
    depth, core = where_ref[0], where_ref[2]
    copies = placing(late, places(where_ref)[EARLY:], t_ref, sem)
    for copy in copies:
        copy.start()
    psi_copy = pltpu.make_async_copy(psi_hbm, psi_ref, psi_sem)
    psi_copy.start()
    chi_ref[...] = u_ref[...]
    for copy in copies:
        copy.wait()

    def body(i, _):
        j = SLICES - 1 - i
        hues = [(j + e) & 3 for e in range(COLOURS)]

        def rows_of(q):
            tiles = [
                t_ref[hues[(x + 2 * yl) & 3], c, j, yl, q] for c in range(2) for x in range(4) for yl in range(4)
            ]
            return jnp.concatenate(tiles, axis=0)

        chi = []
        for h in range(2):
            u = chi_ref[h]
            ur, ui = u[:, :HALF], u[:, HALF:]
            tr, ti = rows_of(h), rows_of(2 + h)
            chi.append(jnp.concatenate([ur * tr + ui * ti, ui * tr - ur * ti], axis=1))
        chi_ref[0], chi_ref[1] = propagate(*chi, table_ref, kc_ref, ks_ref)
        return 0

    lax.fori_loop(0, SLICES - 1 - depth, body, 0)

    psi_copy.wait()
    for h in range(2):
        lanes = slice(h * HALF, (h + 1) * HALF)
        u = chi_ref[h]
        ur, ui = u[:, :HALF], u[:, HALF:]
        pr, pi = held(psi_ref, 0, h), held(psi_ref, 1, h)
        for part, g in enumerate((ur * pr + ui * pi, ui * pr - ur * pi)):
            first, second = g[:HALF], g[HALF:]
            own_ref[:, part, :, lanes] = jnp.where(core == 0, first, second).reshape(16, 8, HALF)
            send_ref[:, part, :, lanes] = jnp.where(core == 0, second, first).reshape(16, 8, HALF)


VMEM = pl.BlockSpec(memory_space=pltpu.VMEM)
SMEM = pl.BlockSpec(memory_space=pltpu.SMEM)
ANY = pl.BlockSpec(memory_space=pl.ANY)


def begin(order, cotangent, kernel_phase):
    field = jax.ShapeDtypeStruct((2, N, N), F32)
    table = jax.ShapeDtypeStruct((2, HALF, N), F32)
    return pl.pallas_call(
        begin_kernel,
        out_shape=(field, table, table),
        in_specs=[SMEM] + [VMEM] * 3,
        out_specs=(VMEM,) * 3,
        compiler_params=pltpu.CompilerParams(vmem_limit_bytes=10 << 20),
        cost_estimate=pl.CostEstimate(flops=2_000_000_000, bytes_accessed=4 << 20, transcendentals=1 << 17),
        name="begin",
    )(order, cotangent.reshape(2, 16, 2, 8, N), kernel_phase, jnp.asarray(tables()))


PLACED = (COLOURS, 2, SLICES, 4, 4, 8, HALF)


def place(where, arrays):
    return pl.pallas_call(
        place_kernel,
        out_shape=pltpu.VMEM(PLACED, F32),
        in_specs=[SMEM] + [ANY] * EARLY,
        out_specs=VMEM,
        scratch_shapes=[pltpu.SemaphoreType.DMA],
        compiler_params=pltpu.CompilerParams(vmem_limit_bytes=2 << 20),
        cost_estimate=pl.CostEstimate(flops=0, bytes_accessed=10 << 20, transcendentals=0),
        name="place",
    )(where, *arrays)


def chain(where, begun, psi, placed, late):
    part = jax.ShapeDtypeStruct((16, 2, 8, N), F32)
    own, send_, _ = pl.pallas_call(
        chain_kernel,
        out_shape=(part, part, pltpu.VMEM(PLACED, F32)),
        in_specs=[SMEM] + [VMEM] * 4 + [ANY, VMEM] + [ANY] * (8 - EARLY),
        out_specs=(VMEM,) * 3,
        input_output_aliases={6: 2},
        scratch_shapes=[
            pltpu.VMEM((2, N, N), F32),
            pltpu.VMEM((2, 16, 2, 8, N), F32),
            pltpu.SemaphoreType.DMA,
            pltpu.SemaphoreType.DMA,
        ],
        compiler_params=pltpu.CompilerParams(vmem_limit_bytes=10 << 20),
        name="chain",
    )(where, *begun, jnp.asarray(tables()), psi.reshape(2, 16, 2, 8, N), placed, *late)
    return own, send_


def send(value, target):
    pairs = []
    for source in range(int(np.prod(SIZES))):
        yh, z, x, yl, c = (int(v) for v in np.unravel_index(source, SIZES))
        y, z, x, c = target(yh * 4 + yl, z, x, c)
        y %= 8
        pairs.append((source, int(np.ravel_multi_index((y // 4, z % 8, x % 4, y % 4, c), SIZES))))
    return lax.ppermute(value, AXES, pairs)


def colour_groups():
    groups = {}
    for yh, z, yl, x, c in np.ndindex(2, 8, 4, 4, 2):
        device = int(np.ravel_multi_index((yh, z, x, yl, c), SIZES))
        groups.setdefault(((x + 2 * yl + z) % COLOURS, c), []).append(device)
    return [groups[key] for key in sorted(groups)]


def per_device(amplitude, phase, kernel_phase, entry_field, cotangent):
    yh, z, x, yl, c = (lax.axis_index(a) for a in AXES)
    where = jnp.stack([yh * 8 + z, lax.rem(x + 2 * yl + z, 4), c]).astype(jnp.int32)
    own = lax.all_to_all(prepare(amplitude, phase), AXES, 0, 0, axis_index_groups=colour_groups())
    begun = begin(where, cotangent.reshape(2, N, N), kernel_phase)
    own, begun = lax.optimization_barrier((own, begun))
    own = own.reshape(SLICES, 4, 4, 8, HALF)
    sign = (1, -1)

    def partner(v):
        return send(v, lambda y, z, x, c: (y, z, x, 1 - c))

    from_x = send(own, lambda y, z, x, c: (y, z, x + sign[c], c))
    from_y = send(own, lambda y, z, x, c: (y + sign[c], z, x, c))
    from_z = send(own, lambda y, z, x, c: (y, z + sign[1 - c], x, 1 - c))
    theirs = partner(own)
    their_x = partner(from_x)
    their_y = partner(from_y)
    their_z = partner(from_z)
    placed = place(where, (own, theirs, from_x, from_y, from_z))
    psi = entry_field.reshape(2, N, N)
    mine, others = chain(where, begun, psi, placed, (their_x, their_y, their_z))
    parts = lax.all_to_all(mine + partner(others), ("x", "yl"), 0, 0)
    return (jnp.sum(parts, axis=0) * (1.0 / math.sqrt(32)))[:, None]


def solution(mesh):
    fine = Mesh(mesh.devices.reshape(SIZES), AXES)
    depth, illum = ("yh", "z"), ("x", "yl", "c")
    return jax.shard_map(
        per_device,
        mesh=fine,
        in_specs=(
            P(depth, illum, None),
            P(depth, illum, None),
            P(),
            P(None, depth, illum, None, None),
            P(None, illum, None, None),
        ),
        out_specs=P(None, depth, illum, None),
        check_vma=False,
    )
```

```python
import functools
import math

import jax
import jax.numpy as jnp
import numpy as np
from jax import lax
from jax.experimental import pallas as pl
from jax.experimental.pallas import tpu as pltpu
from jax.sharding import Mesh, PartitionSpec as P

AXES = ("yh", "z", "x", "yl", "c")
SIZES = (2, 8, 4, 4, 2)
N = 256
HALF = 128
SLICES = 16
COLOURS = 4
PEERS = 64
BLOCK = 4
FIRST, NEXT, LAST = (0, 1), (2, 3, 4, 6, 7), (5,)
F32 = jnp.float32
BF16 = jnp.bfloat16


def _real_form(angle):
    c, s = np.cos(angle), np.sin(angle)
    return np.block([[c, -s], [s, c]])


def _split_np(m):
    hi = m.astype(BF16)
    return hi, (m - hi.astype(np.float64)).astype(BF16)


@functools.cache
def tables():
    n = np.arange(HALF)
    even = _real_form(2 * np.pi * ((n[:, None] * n[None, :]) % HALF) / HALF)
    odd = _real_form(2 * np.pi * ((n[:, None] * (2 * n[None, :] + 1)) % N) / N)
    core, x, yl, r = np.meshgrid(np.arange(2), np.arange(2), np.arange(4), np.arange(8), indexing="ij")
    order = (x * 64 + yl * 16 + core * 8 + r).reshape(-1)
    both = np.concatenate([order, order + HALF])
    right, left = [], []
    for m in (even, odd, even.T, odd.T):
        hi, lo = _split_np(m)
        right.append(np.stack([hi, lo]))
    for m in (even.T[:, both], odd.T[:, both], even[both, :], odd[both, :]):
        hi, lo = _split_np(m)
        left.append(np.stack([hi, lo]))
    return np.stack(right + left)


def sincos(angle):
    turns = jnp.round(angle * (2.0 / math.pi))
    r = ((angle - turns * 1.5703125) - turns * 4.837512969970703125e-4) - turns * 7.54978995489188216e-8
    quadrant = turns.astype(jnp.int32)
    z = r * r
    sine = r + r * z * (-1.6666654611e-1 + z * (8.3321608736e-3 - z * 1.9515295891e-4))
    cosine = 1.0 - 0.5 * z + z * z * (4.166664568298827e-2 + z * (-1.388731625493765e-3 + z * 2.443315711809948e-5))
    odd = (quadrant & 1) == 1
    s, c = jnp.where(odd, cosine, sine), jnp.where(odd, sine, cosine)
    s = jnp.where((quadrant & 2) == 2, -s, s)
    c = jnp.where(((quadrant + 1) & 2) == 2, -c, c)
    return s, c


def prepare_kernel(amp_ref, phase_ref, out_hbm, block_ref, sem):
    amp = amp_ref[0]
    sine, cosine = sincos(phase_ref[0])
    re, im = amp * cosine, amp * sine
    for q, tile in enumerate((re[:, :HALF], re[:, HALF:], im[:, :HALF], im[:, HALF:])):
        for chip in range(BLOCK):
            block_ref[chip, q] = tile
    copies = [
        pltpu.make_async_copy(block_ref, out_hbm.at[first : first + BLOCK], sem) for first in range(0, PEERS, BLOCK)
    ]
    for copy in copies:
        copy.start()
    for copy in copies:
        copy.wait()


def prepare(amplitude, phase):
    return pl.pallas_call(
        prepare_kernel,
        out_shape=jax.ShapeDtypeStruct((PEERS, 4, 8, HALF), F32),
        out_specs=pl.BlockSpec(memory_space=pl.ANY),
        scratch_shapes=[pltpu.VMEM((BLOCK, 4, 8, HALF), F32), pltpu.SemaphoreType.DMA],
        name="prepare",
    )(amplitude, phase)


def split(value):
    hi = value.astype(BF16)
    return hi, (value - hi.astype(F32)).astype(BF16)


def dot_right(value, table):
    hi, lo = split(value)
    wide = jnp.concatenate([table[0], table[0], table[1]], axis=0)
    return jnp.dot(jnp.concatenate([hi, lo, hi], axis=1), wide, preferred_element_type=F32)


def dot_left(table, value):
    hi, lo = split(value)
    wide = jnp.concatenate([table[0], table[0], table[1]], axis=1)
    return jnp.dot(wide, jnp.concatenate([hi, lo, hi], axis=0), preferred_element_type=F32)


def propagate(chi_l, chi_r, table_ref, kc_ref, ks_ref):
    ye = dot_right(chi_l + chi_r, table_ref[0])
    yo = dot_right(chi_l - chi_r, table_ref[1])
    re = jnp.concatenate([ye[:, :HALF], yo[:, :HALF]], axis=1)
    im = jnp.concatenate([ye[:, HALF:], yo[:, HALF:]], axis=1)

    def first(v):
        return jnp.concatenate([v[0:64], v[128:192]], axis=0)

    def second(v):
        return jnp.concatenate([v[64:128], v[192:256]], axis=0)

    a = jnp.concatenate([first(re), first(im)], axis=0)
    b = jnp.concatenate([second(re), second(im)], axis=0)
    freqs = [dot_left(table_ref[4 + i], mixed) for i, mixed in enumerate((a + b, a - b))]
    out = []
    for i, freq in enumerate(freqs):
        fr, fi = freq[:HALF], freq[HALF:]
        c, s = kc_ref[i], ks_ref[i]
        weighted = jnp.concatenate([fr * c + fi * s, fi * c - fr * s], axis=0)
        out.append(dot_left(table_ref[6 + i], weighted))
    top, low = out[0] + out[1], out[0] - out[1]

    def rows(part):
        t, l = top[part * HALF : (part + 1) * HALF], low[part * HALF : (part + 1) * HALF]
        return jnp.concatenate([t[:64], l[:64], t[64:], l[64:]], axis=0)

    re, im = rows(0), rows(1)
    ue = dot_right(jnp.concatenate([re[:, :HALF], im[:, :HALF]], axis=1), table_ref[2])
    uo = dot_right(jnp.concatenate([re[:, HALF:], im[:, HALF:]], axis=1), table_ref[3])
    return ue + uo, ue - uo


def three(value):
    hi = value.astype(BF16)
    rest = value - hi.astype(F32)
    mid = rest.astype(BF16)
    return hi, mid, (rest - mid.astype(F32)).astype(BF16)


def held(ref, part, half):
    lanes = slice(half * HALF, (half + 1) * HALF)
    return jnp.concatenate([ref[part, :, c, :, lanes].reshape(HALF, HALF) for c in range(2)], axis=0)


def begin_kernel(order_ref, cot_ref, kern_ref, table_ref, u_ref, kc_ref, ks_ref):
    del order_ref
    row = lax.broadcasted_iota(jnp.int32, (N, N), 0)
    col = lax.broadcasted_iota(jnp.int32, (N, N), 1)
    picks = jnp.where(col == jnp.where(row < HALF, 2 * row, 2 * row - (N - 1)), 1.0, 0.0).astype(BF16)
    picks_t = jnp.where(row == jnp.where(col < HALF, 2 * col, 2 * col - (N - 1)), 1.0, 0.0).astype(BF16)
    angle = kern_ref[...]
    angle = sum(jnp.dot(picks, p, preferred_element_type=F32) for p in three(angle))
    angle = sum(jnp.dot(p, picks_t, preferred_element_type=F32) for p in three(angle))
    scale = 1.0 / (N * N)
    sine, cosine = sincos(angle)
    kc_ref[...] = (cosine * scale).reshape(2, HALF, N)
    ks_ref[...] = (sine * scale).reshape(2, HALF, N)
    fields = (jnp.concatenate([held(cot_ref, 0, h), held(cot_ref, 1, h)], axis=1) for h in range(2))
    u_ref[0], u_ref[1] = propagate(*fields, table_ref, kc_ref, ks_ref)


def places(where_ref):
    colour, core = where_ref[1], where_ref[2]
    other = 1 - core
    near = lax.rem(colour + jnp.where(core == 0, 3, 1), COLOURS)
    far = lax.rem(colour + jnp.where(core == 0, 1, 3), COLOURS)
    across = lax.rem(colour + 2, COLOURS)
    return (
        (colour, core), (colour, other),
        (near, core), (across, core), (near, other),
        (far, other), (across, other), (far, core),
    )


def placing(arrays, which, where_ref, t_ref, sem):
    used = slice(1, SLICES)
    slots = places(where_ref)
    return [
        pltpu.make_async_copy(ref.at[used], t_ref.at[slots[i][0], slots[i][1], used], sem)
        for ref, i in zip(arrays, which)
    ]


def place_kernel(which, where_ref, *rest):
    arrays, (t_ref, sem) = rest[: len(which)], rest[-2:]
    copies = placing(arrays, which, where_ref, t_ref, sem)
    for copy in copies:
        copy.start()
    for copy in copies:
        copy.wait()


def chain_kernel(where_ref, u_ref, kc_ref, ks_ref, table_ref, psi_hbm, placed_ref, *rest):
    del placed_ref
    last, (own_ref, send_ref, t_ref, chi_ref, psi_ref, sem, psi_sem) = rest[: len(LAST)], rest[len(LAST) :]
    depth, core = where_ref[0], where_ref[2]
    copies = placing(last, LAST, where_ref, t_ref, sem)
    for copy in copies:
        copy.start()
    psi_copy = pltpu.make_async_copy(psi_hbm, psi_ref, psi_sem)
    psi_copy.start()
    chi_ref[...] = u_ref[...]
    for copy in copies:
        copy.wait()

    def body(i, _):
        j = SLICES - 1 - i
        hues = [(j + e) & 3 for e in range(COLOURS)]

        def rows_of(q):
            tiles = [
                t_ref[hues[(x + 2 * yl) & 3], c, j, yl, q] for c in range(2) for x in range(4) for yl in range(4)
            ]
            return jnp.concatenate(tiles, axis=0)

        chi = []
        for h in range(2):
            u = chi_ref[h]
            ur, ui = u[:, :HALF], u[:, HALF:]
            tr, ti = rows_of(h), rows_of(2 + h)
            chi.append(jnp.concatenate([ur * tr + ui * ti, ui * tr - ur * ti], axis=1))
        chi_ref[0], chi_ref[1] = propagate(*chi, table_ref, kc_ref, ks_ref)
        return 0

    lax.fori_loop(0, SLICES - 1 - depth, body, 0)

    psi_copy.wait()
    for h in range(2):
        lanes = slice(h * HALF, (h + 1) * HALF)
        u = chi_ref[h]
        ur, ui = u[:, :HALF], u[:, HALF:]
        pr, pi = held(psi_ref, 0, h), held(psi_ref, 1, h)
        for part, g in enumerate((ur * pr + ui * pi, ui * pr - ur * pi)):
            first, second = g[:HALF], g[HALF:]
            own_ref[:, part, :, lanes] = jnp.where(core == 0, first, second).reshape(16, 8, HALF)
            send_ref[:, part, :, lanes] = jnp.where(core == 0, second, first).reshape(16, 8, HALF)


VMEM = pl.BlockSpec(memory_space=pltpu.VMEM)
SMEM = pl.BlockSpec(memory_space=pltpu.SMEM)
ANY = pl.BlockSpec(memory_space=pl.ANY)


def begin(order, cotangent, kernel_phase):
    field = jax.ShapeDtypeStruct((2, N, N), F32)
    table = jax.ShapeDtypeStruct((2, HALF, N), F32)
    return pl.pallas_call(
        begin_kernel,
        out_shape=(field, table, table),
        in_specs=[SMEM] + [VMEM] * 3,
        out_specs=(VMEM,) * 3,
        compiler_params=pltpu.CompilerParams(vmem_limit_bytes=10 << 20),
        cost_estimate=pl.CostEstimate(flops=2_000_000_000, bytes_accessed=4 << 20, transcendentals=1 << 17),
        name="begin",
    )(order, cotangent.reshape(2, 16, 2, 8, N), kernel_phase, jnp.asarray(tables()))


PLACED = (COLOURS, 2, SLICES, 4, 4, 8, HALF)


def place(where, gathered, which, placed=None):
    before = () if placed is None else (placed,)
    return pl.pallas_call(
        functools.partial(place_kernel, which),
        out_shape=pltpu.VMEM(PLACED, F32),
        in_specs=[SMEM] + [ANY] * len(which) + [VMEM] * len(before),
        out_specs=VMEM,
        input_output_aliases={1 + len(which): 0} if before else {},
        scratch_shapes=[pltpu.SemaphoreType.DMA],
        compiler_params=pltpu.CompilerParams(vmem_limit_bytes=2 << 20),
        cost_estimate=pl.CostEstimate(flops=0, bytes_accessed=len(which) << 21, transcendentals=0),
        name="place",
    )(where, *(gathered[i] for i in which), *before)


def chain(where, begun, psi, placed, gathered):
    part = jax.ShapeDtypeStruct((16, 2, 8, N), F32)
    own, send_, _ = pl.pallas_call(
        chain_kernel,
        out_shape=(part, part, pltpu.VMEM(PLACED, F32)),
        in_specs=[SMEM] + [VMEM] * 4 + [ANY, VMEM] + [ANY] * len(LAST),
        out_specs=(VMEM,) * 3,
        input_output_aliases={6: 2},
        scratch_shapes=[
            pltpu.VMEM((2, N, N), F32),
            pltpu.VMEM((2, 16, 2, 8, N), F32),
            pltpu.SemaphoreType.DMA,
            pltpu.SemaphoreType.DMA,
        ],
        compiler_params=pltpu.CompilerParams(vmem_limit_bytes=10 << 20),
        name="chain",
    )(where, *begun, jnp.asarray(tables()), psi.reshape(2, 16, 2, 8, N), placed, *(gathered[i] for i in LAST))
    return own, send_


def send(value, target):
    pairs = []
    for source in range(int(np.prod(SIZES))):
        yh, z, x, yl, c = (int(v) for v in np.unravel_index(source, SIZES))
        y, z, x, c = target(yh * 4 + yl, z, x, c)
        y %= 8
        pairs.append((source, int(np.ravel_multi_index((y // 4, z % 8, x % 4, y % 4, c), SIZES))))
    return lax.ppermute(value, AXES, pairs)


def colour_groups():
    groups = {}
    for yh, z, yl, x, c in np.ndindex(2, 8, 4, 4, 2):
        device = int(np.ravel_multi_index((yh, z, x, yl, c), SIZES))
        groups.setdefault(((x + 2 * yl + z) % COLOURS, c), []).append(device)
    return [groups[key] for key in sorted(groups)]


def per_device(amplitude, phase, kernel_phase, entry_field, cotangent):
    yh, z, x, yl, c = (lax.axis_index(a) for a in AXES)
    where = jnp.stack([yh * 8 + z, lax.rem(x + 2 * yl + z, 4), c]).astype(jnp.int32)
    own = lax.all_to_all(prepare(amplitude, phase), AXES, 0, 0, axis_index_groups=colour_groups())
    begun = begin(where, cotangent.reshape(2, N, N), kernel_phase)
    own, begun = lax.optimization_barrier((own, begun))
    own = own.reshape(SLICES, 4, 4, 8, HALF)
    sign = (1, -1)

    def partner(v):
        return send(v, lambda y, z, x, c: (y, z, x, 1 - c))

    from_x = send(own, lambda y, z, x, c: (y, z, x + sign[c], c))
    from_y = send(own, lambda y, z, x, c: (y + sign[c], z, x, c))
    from_z = send(own, lambda y, z, x, c: (y, z + sign[1 - c], x, 1 - c))
    theirs = partner(own)
    their_x = partner(from_x)
    their_y = partner(from_y)
    their_z = partner(from_z)
    gathered = (own, theirs, from_x, from_y, from_z, their_x, their_y, their_z)
    placed = place(where, gathered, FIRST)
    placed = place(where, gathered, NEXT, placed)
    psi = entry_field.reshape(2, N, N)
    mine, others = chain(where, begun, psi, placed, gathered)
    parts = lax.all_to_all(mine + partner(others), ("x", "yl"), 0, 0)
    return (jnp.sum(parts, axis=0) * (1.0 / math.sqrt(32)))[:, None]


def solution(mesh):
    fine = Mesh(mesh.devices.reshape(SIZES), AXES)
    depth, illum = ("yh", "z"), ("x", "yl", "c")
    return jax.shard_map(
        per_device,
        mesh=fine,
        in_specs=(
            P(depth, illum, None),
            P(depth, illum, None),
            P(),
            P(None, depth, illum, None, None),
            P(None, illum, None, None),
        ),
        out_specs=P(None, depth, illum, None),
        check_vma=False,
    )
```
